256 devices in a mesh: row: 8 (over z_lo, core), col: 32 (over z_hi, y, x).
Axes of the slice: x: 4, y: 4, z: 8 (z_hi: 2, z_lo: 4; z = z_hi * 4 + z_lo), core: 2. Of those that a mesh axis runs over, the one named last changes fastest.
Arguments:
- tokens: bfloat16 [1024, 12288], P('col', 'row'), may hold values from -6 to 6
- up_weight: bfloat16 [12288, 24576], P('row', 'col'), may hold values from -0.109375 to 0.109375
- down_weight: bfloat16 [24576, 12288], P('col', 'row'), may hold values from -0.078125 to 0.078125
- cotangent: bfloat16 [1024, 12288], P('col', 'row'), may hold values from -6 to 6
- up_pattern: int32 [96, 192], P('row', 'col'), may hold values 0 or 1
- down_pattern: int32 [192, 96], P('col', 'row'), may hold values 0 or 1
Outputs:
- input_grad: bfloat16 [1024, 12288], P('col', 'row')
- up_grad: bfloat16 [12288, 24576], P('row', 'col')
- down_grad: bfloat16 [24576, 12288], P('col', 'row')
The draws below stay inside these ranges and needn't reach their ends.
All inputs are finite; a program needn't handle non-finite values. No bound on the sum of `up_pattern` or of `down_pattern` on one device may be relied on, other than what follows from the above.
Results may differ from the reference program's by a relative error of at most 0.015.
Values may be sent and summed in bfloat16 or wider, within the bound.
A program may use at most 128 MiB of HBM per device.

```python
import jax
import jax.numpy as jnp
from jax import lax

D = 12288
FF = 24576
BLOCK = 128
TOKENS = 1024
DB = 96
FB = 192


def touch_ends(drawn, own_key, low, largest):
    spot = [jax.random.randint(jax.random.fold_in(own_key, axis), (), 0, length) for axis, length in enumerate(drawn.shape)]
    widest = drawn.shape.index(max(drawn.shape))
    next_to = spot[:widest] + [(spot[widest] + 1) % drawn.shape[widest]] + spot[widest + 1:]
    return drawn.at[tuple(spot)].set(low).at[tuple(next_to)].set(largest)


def block_scale(stream_key, extent, split, low, largest):
    loudness = 1.0
    for position, blocks in split:
        heights = jax.random.uniform(jax.random.fold_in(jax.random.fold_in(stream_key, 6), position), (blocks,), jnp.float32, low / len(split), largest / len(split))
        loudness = loudness * jnp.repeat(jnp.exp(heights), extent[position] // blocks).reshape((-1,) + (1,) * (len(extent) - 1 - position))
    return loudness


def bell_draw(key, shape, width, reach, pieces=(), held_as=jnp.bfloat16):
    values = jax.random.normal(key, shape, jnp.float32) * width
    if len(pieces) > 0:
        values = block_scale(key, shape, pieces, -0.22, 0.18) * values
    return jnp.clip(values, min=-reach, max=reach).astype(held_as)


def setup_inputs(seed: int = 0) -> dict:
    streams_of = jax.random.split(jax.random.key(seed), 7)
    tokens = bell_draw(streams_of[0], (TOKENS, D), 1.0, 6.0, ((0, 32), (1, 8)))
    up_weight = bell_draw(streams_of[1], (D, FF), (D // 4) ** -0.5, 0.109375, ((0, 8), (1, 32)))
    down_weight = bell_draw(streams_of[2], (FF, D), (FF // 4) ** -0.5, 0.078125, ((0, 32), (1, 8)))
    cotangent = bell_draw(streams_of[3], (TOKENS, D), 1.0, 6.0, ((0, 32), (1, 8)))
    up_pattern = touch_ends((jax.random.randint(streams_of[4], (DB, FB), 0, 4) < 1).astype(jnp.int32), jax.random.fold_in(streams_of[4], 1), 0, 1)
    down_pattern = touch_ends((jax.random.randint(streams_of[5], (FB, DB), 0, 4) < 1).astype(jnp.int32), jax.random.fold_in(streams_of[5], 1), 0, 1)
    return {"tokens": tokens, "up_weight": up_weight, "down_weight": down_weight, "cotangent": cotangent, "up_pattern": up_pattern, "down_pattern": down_pattern}


half_root = 0.7071067811865476
inv_root_tau = 0.3989422804014327

def widen(pattern):
    return jnp.repeat(jnp.repeat(pattern, BLOCK, axis=0), BLOCK, axis=1).astype(jnp.bfloat16)

def reference(tokens, up_weight, down_weight, cotangent, up_pattern, down_pattern):
    up_mask = widen(up_pattern)
    down_mask = widen(down_pattern)
    up_eff = up_weight * up_mask
    down_eff = down_weight * down_mask
    pre = jnp.dot(tokens, up_eff, preferred_element_type=jnp.float32)
    dact = lax.dot_general(cotangent, down_eff, (((1,), (1,)), ((), ())), preferred_element_type=jnp.float32)
    cdf = 0.5 * (1.0 + jax.scipy.special.erf(pre * half_root))
    dens = jnp.exp(-0.5 * pre * pre) * inv_root_tau
    active = (pre * cdf).astype(jnp.bfloat16)
    dhid = (dact * (cdf + pre * dens)).astype(jnp.bfloat16)
    input_grad = lax.dot_general(dhid, up_eff, (((1,), (1,)), ((), ())), preferred_element_type=jnp.float32).astype(jnp.bfloat16)
    factor = 1.0 / jnp.sqrt(jnp.float32(TOKENS))
    up_grad = lax.dot_general(tokens, dhid, (((0,), (0,)), ((), ())), preferred_element_type=jnp.float32)
    up_grad = (up_grad * up_mask.astype(jnp.float32) * factor).astype(jnp.bfloat16)
    down_grad = lax.dot_general(active, cotangent, (((0,), (0,)), ((), ())), preferred_element_type=jnp.float32)
    down_grad = (down_grad * down_mask.astype(jnp.float32) * factor).astype(jnp.bfloat16)
    return (input_grad, up_grad, down_grad)
```

```python
import jax
import jax.numpy as jnp
from jax import lax
from jax.experimental import pallas as pl
from jax.experimental.pallas import tpu as pltpu
from jax.sharding import PartitionSpec as P

MESH = pl.DeviceIdType.MESH
HALF_ROOT = 0.7071067811865476
INV_ROOT_TAU = 0.3989422804014327
BF = jnp.bfloat16
F32 = jnp.float32
NT = (((1,), (1,)), ((), ()))
TN = (((0,), (0,)), ((), ()))


def kernel(
    tok, upw, dnw, cot, upp, dnp, ig_out, ug_out, dg_out,
    T, G, U, D, PS, XS, XR, RSS, RSR, AD, IG, RA, RB, CS, R1, R1B, RC, RD, CS2, R2, ZS, ZR, UG, DG, OUT,
    lsem, ags, agr, zxs, zxr, xs, xr, rss, rsr, ads, adr, acs, acr, igs, igr, zss, zsr,
):
    r = lax.axis_index("row")
    q = lax.axis_index("col")
    zl, c = r // 2, lax.rem(r, 2)
    zh = q // 16
    y = lax.rem(q // 4, 4)
    x = lax.rem(q, 4)
    oc = 1 - c

    def m4(v):
        return lax.rem(v, 4)

    xp = (r, zh * 16 + y * 4 + m4(x + 1))
    xm = (r, zh * 16 + y * 4 + m4(x + 3))
    yp = (r, zh * 16 + m4(y + 1) * 4 + x)
    ym = (r, zh * 16 + m4(y + 3) * 4 + x)
    zz = (r, (1 - zh) * 16 + y * 4 + x)
    co = (zl * 2 + oc, q)
    zp = (m4(zl + 1) * 2 + c, q)
    zm = (m4(zl + 3) * 2 + c, q)

    o0 = m4(x + y)
    locals_ = [
        pltpu.make_async_copy(tok, T.at[0, o0, :, y], lsem.at[0]),
        pltpu.make_async_copy(cot, G.at[0, o0, :, y], lsem.at[1]),
        pltpu.make_async_copy(upw, U, lsem.at[2]),
        pltpu.make_async_copy(dnw, D, lsem.at[3]),
    ]
    for d in locals_:
        d.start()

    barrier = pltpu.get_barrier_semaphore()
    for dev in (xp, xm, yp, ym, zz, co, zp, zm):
        pl.semaphore_signal(barrier, inc=1, device_id=dev, device_id_type=MESH)
    locals_[0].wait()
    locals_[1].wait()
    pl.semaphore_wait(barrier, 8)

    pending = []

    def rcopy(src, dst, ss, rs, dev):
        return pltpu.make_async_remote_copy(
            src_ref=src, dst_ref=dst, send_sem=ss, recv_sem=rs, device_id=dev, device_id_type=MESH
        )

    def send(make, cond=None):
        if cond is None:
            make().start()
        else:
            @pl.when(cond)
            def _():
                make().start()
        pending.append((cond, make))

    def arrive(ref, ss, rs):
        rcopy(ref, ref, ss, rs, co).wait_recv()

    class Gather:
        def __init__(self, A, arr, rho):
            self.A, self.arr, self.rho = A, arr, rho
            self.fp, self.fm, self.sp, self.sm = (xp, xm, yp, ym) if arr == 0 else (yp, ym, xp, xm)

        def ref(self, da, db, h=None):
            da, db = da % 4, db % 4
            xx, yy = (m4(x + da), m4(y + db)) if self.arr == 0 else (m4(x + db), m4(y + da))
            o = m4(xx + yy)
            if h is None:
                return self.A.at[self.rho, o, :, yy]
            return self.A.at[self.rho, o, h, yy]

        def put(self, k, ref, dev):
            ss, rs = ags.at[self.arr, self.rho, k], agr.at[self.arr, self.rho, k]
            send(lambda: rcopy(ref, ref, ss, rs, dev))

        def get(self, k, ref):
            arrive(ref, ags.at[self.arr, self.rho, k], agr.at[self.arr, self.rho, k])

        def start(self):
            own = self.ref(0, 0)
            self.put(0, own, self.fp)
            self.put(1, own, self.fm)
            self.put(2, own, self.sp)
            self.put(3, own, self.sm)

        def step2(self):
            self.get(0, self.ref(-1, 0))
            self.put(4, self.ref(-1, 0, 0), self.fp)
            self.put(5, self.ref(-1, 0), self.sp)
            self.put(6, self.ref(-1, 0), self.sm)
            self.get(1, self.ref(1, 0))
            self.put(7, self.ref(1, 0, 1), self.fm)
            self.put(8, self.ref(1, 0), self.sp)
            self.put(9, self.ref(1, 0), self.sm)

        def step3(self):
            self.get(4, self.ref(2, 0, 0))
            self.get(7, self.ref(2, 0, 1))
            self.put(10, self.ref(2, 0), self.sp)
            self.put(11, self.ref(2, 0), self.sm)

        def step4a(self):
            self.get(2, self.ref(0, -1))
            self.put(12, self.ref(0, -1), self.sp)
            self.get(6, self.ref(-1, 1))
            self.put(13, self.ref(-1, 1), self.sm)

        def step4b(self):
            self.get(8, self.ref(1, -1))
            self.put(14, self.ref(1, -1), self.sp)
            self.get(11, self.ref(2, 1))
            self.put(15, self.ref(2, 1), self.sm)

        def finish(self):
            self.get(3, self.ref(0, 1))
            self.get(5, self.ref(-1, -1))
            self.get(9, self.ref(1, 1))
            self.get(10, self.ref(2, -1))
            self.get(12, self.ref(0, 2))
            self.get(13, self.ref(-1, 2))
            self.get(14, self.ref(1, 2))
            self.get(15, self.ref(2, 2))

    gt0, gg0 = Gather(T, 0, 0), Gather(G, 1, 0)
    gt1, gg1 = Gather(T, 0, 1), Gather(G, 1, 1)

    def across(A, k):
        src, dst = A.at[0, o0, :, y], A.at[1, o0, :, y]
        send(lambda: rcopy(src, dst, zxs.at[k], zxr.at[k], zz))

    def across_wait(A, k):
        arrive(A.at[1, o0, :, y], zxs.at[k], zxr.at[k])

    def row_a(i):
        rho, f = i // 3, i % 3
        cols = slice(f * 256, (f + 1) * 256)
        for o in range(0, 4, 2):
            t = T[rho, o:o + 2].reshape(256, 1536)
            pre = jnp.dot(t, U[:, cols], preferred_element_type=F32)
            PS[i, 0, o:o + 2] = pre.reshape(2, 2, 4, 16, 256)
            g = G[rho, o:o + 2].reshape(256, 1536)
            dact = lax.dot_general(g, D[cols, :], NT, preferred_element_type=F32)
            PS[i, 1, o:o + 2] = dact.reshape(2, 2, 4, 16, 256)
        XS[i] = PS[i, :, :, oc].astype(BF)
        send(lambda: rcopy(XS.at[i], XR.at[i], xs.at[i], xr.at[i], co))

    def rs_send(i, way, k, cond):
        dev = zp if way == 0 else zm
        send(
            lambda: rcopy(
                RSS.at[i, way, k - 1], RSR.at[i, way, k - 1], rss.at[i, way, k - 1], rsr.at[i, way, k - 1], dev
            ),
            cond,
        )

    def rs_arrive(i, way, k):
        arrive(RSR.at[i, way, k - 1], rss.at[i, way, k - 1], rsr.at[i, way, k - 1])

    def row_b(i):
        arrive(XR.at[i], xs.at[i], xr.at[i])
        PS[i, :, :, c] = PS[i, :, :, c] + XR[i].astype(F32)

        @pl.when(zl == 0)
        def _():
            for k in (3, 2, 1):
                RSS[i, 0, k - 1] = PS[i, :, k, c].astype(BF)

        @pl.when(zl == 3)
        def _():
            for k in (3, 2, 1):
                RSS[i, 1, k - 1] = PS[i, :, 3 - k, c].astype(BF)

        for k in (3, 2, 1):
            rs_send(i, 0, k, zl == 0)
            rs_send(i, 1, k, zl == 3)

    def row_c(i, k):
        right = jnp.logical_and(zl >= 1, zl + k <= 3)
        left = jnp.logical_and(zl <= 2, zl - k >= 0)

        @pl.when(right)
        def _():
            rs_arrive(i, 0, k + 1)
            RSS[i, 0, k - 1] = (PS[i, :, zl + k, c] + RSR[i, 0, k].astype(F32)).astype(BF)

        rs_send(i, 0, k, right)

        @pl.when(left)
        def _():
            rs_arrive(i, 1, k + 1)
            RSS[i, 1, k - 1] = (PS[i, :, zl - k, c] + RSR[i, 1, k].astype(F32)).astype(BF)

        rs_send(i, 1, k, left)

    has_left, has_right = zl >= 1, zl <= 2

    def ad_line(i, way, d, block, cond):
        dev = zp if way == 0 else zm
        f_rho = (i // 3, i % 3)
        send(
            lambda: rcopy(
                AD.at[f_rho[0], f_rho[1], block, c], AD.at[f_rho[0], f_rho[1], block, c],
                ads.at[i, way, d - 1], adr.at[i, way, d - 1], dev,
            ),
            cond,
        )

    def ad_core(i, slot, block, cond):
        send(
            lambda: rcopy(
                AD.at[i // 3, i % 3, block, c], AD.at[i // 3, i % 3, block, c], acs.at[i, slot], acr.at[i, slot], co
            ),
            cond,
        )

    def row_d(i):
        rho, f = i // 3, i % 3

        @pl.when(has_left)
        def _():
            rs_arrive(i, 0, 1)
            PS[i, :, zl, c] = PS[i, :, zl, c] + RSR[i, 0, 0].astype(F32)

        @pl.when(has_right)
        def _():
            rs_arrive(i, 1, 1)
            PS[i, :, zl, c] = PS[i, :, zl, c] + RSR[i, 1, 0].astype(F32)

        pre = PS[i, 0, zl, c]
        dact = PS[i, 1, zl, c]
        cdf = 0.5 * (1.0 + lax.erf(pre * HALF_ROOT))
        dens = jnp.exp(-0.5 * pre * pre) * INV_ROOT_TAU
        AD[rho, f, zl, c, 0] = (pre * cdf).astype(BF)
        AD[rho, f, zl, c, 1] = (dact * (cdf + pre * dens)).astype(BF)
        ad_line(i, 0, 1, zl, has_right)
        ad_line(i, 1, 1, zl, has_left)
        ad_core(i, 0, zl, None)

    def row_e(i, d):
        from_left, from_right = zl - d >= 0, zl + d <= 3

        @pl.when(from_left)
        def _():
            arrive(AD.at[i // 3, i % 3, zl - d, c], ads.at[i, 0, d - 1], adr.at[i, 0, d - 1])

        if d < 3:
            ad_line(i, 0, d + 1, zl - d, jnp.logical_and(from_left, has_right))
        ad_core(i, d, zl - d, from_left)

        @pl.when(from_right)
        def _():
            arrive(AD.at[i // 3, i % 3, zl + d, c], ads.at[i, 1, d - 1], adr.at[i, 1, d - 1])

        if d < 3:
            ad_line(i, 1, d + 1, zl + d, jnp.logical_and(from_right, has_left))
        ad_core(i, 3 + d, zl + d, from_right)

    def row_f(i):
        arrive(AD.at[i // 3, i % 3, zl, oc], acs.at[i, 0], acr.at[i, 0])
        for d in (1, 2, 3):
            @pl.when(zl - d >= 0)
            def _():
                arrive(AD.at[i // 3, i % 3, zl - d, oc], acs.at[i, d], acr.at[i, d])

            @pl.when(zl + d <= 3)
            def _():
                arrive(AD.at[i // 3, i % 3, zl + d, oc], acs.at[i, 3 + d], acr.at[i, 3 + d])

    def ig_matmul(rho, h):
        @pl.loop(0, 3)
        def _(n):
            rows = pl.ds(pl.multiple_of(h * 768 + n * 256, 256), 256)
            cols = pl.ds(pl.multiple_of(n * 256, 256), 256)
            for o in range(0, 4, 2):
                acc = jnp.zeros((256, 256), F32)
                for f in range(3):
                    dh = AD[rho, f, o:o + 2, :, 1].reshape(256, 256)
                    acc = acc + lax.dot_general(
                        dh, U[rows, f * 256:(f + 1) * 256], NT, preferred_element_type=F32
                    )
                acc = acc.astype(BF).reshape(2, 2, 4, 16, 256)
                for oo in range(2):
                    for yy in range(4):
                        xx = (o + oo - yy) % 4
                        a, b = (yy, xx) if h == 0 else (xx, yy)
                        IG[rho, h, a, b, :, :, cols] = acc[oo, :, yy]

    class Scatter:
        def __init__(self, rho, h):
            self.rho, self.h = rho, h
            self.fp, self.fm, self.sp, self.sm = (yp, ym, xp, xm) if h == 0 else (xp, xm, yp, ym)
            self.a, self.b = (y, x) if h == 0 else (x, y)

        def put(self, k, src, dst, dev):
            ss, rs = igs.at[self.rho, self.h, k], igr.at[self.rho, self.h, k]
            send(lambda: rcopy(src, dst, ss, rs, dev))

        def get(self, k, ref):
            arrive(ref, igs.at[self.rho, self.h, k], igr.at[self.rho, self.h, k])

        def start(self):
            i = (self.rho, self.h)
            a = self.a
            a1, a2, a3 = m4(a + 1), m4(a + 2), m4(a + 3)
            self.put(0, IG.at[i[0], i[1], a2, 0:2], RA.at[i[0], i[1], 0], self.fp)
            self.put(1, IG.at[i[0], i[1], a2, 2:4], RA.at[i[0], i[1], 1], self.fm)
            self.put(2, IG.at[i[0], i[1], a1, 2:4], RB.at[i[0], i[1], 0, 2:4], self.fp)
            self.put(3, IG.at[i[0], i[1], a3, 0:2], RB.at[i[0], i[1], 1, 0:2], self.fm)

        def step2(self):
            rho, h, a = self.rho, self.h, self.a
            a1, a3 = m4(a + 1), m4(a + 3)
            self.get(0, RA.at[rho, h, 0])
            CS[rho, h, 0] = (IG[rho, h, a1, 0:2].astype(F32) + RA[rho, h, 0].astype(F32)).astype(BF)
            self.put(4, CS.at[rho, h, 0], RB.at[rho, h, 0, 0:2], self.fp)
            self.get(1, RA.at[rho, h, 1])
            CS[rho, h, 1] = (IG[rho, h, a3, 2:4].astype(F32) + RA[rho, h, 1].astype(F32)).astype(BF)
            self.put(5, CS.at[rho, h, 1], RB.at[rho, h, 1, 2:4], self.fm)

        def step3(self):
            rho, h, a, b = self.rho, self.h, self.a, self.b
            self.get(2, RB.at[rho, h, 0, 2:4])
            self.get(3, RB.at[rho, h, 1, 0:2])
            self.get(4, RB.at[rho, h, 0, 0:2])
            self.get(5, RB.at[rho, h, 1, 2:4])
            for k in range(4):
                s = IG[rho, h, a, k].astype(F32) + RB[rho, h, 0, k].astype(F32) + RB[rho, h, 1, k].astype(F32)
                R1[rho, h, k] = s
                R1B[rho, h, k] = s.astype(BF)
            b1, b2, b3 = m4(b + 1), m4(b + 2), m4(b + 3)
            self.put(6, R1B.at[rho, h, b2, 0], RC.at[rho, h, 0], self.sp)
            self.put(7, R1B.at[rho, h, b2, 1], RC.at[rho, h, 1], self.sm)
            self.put(8, R1B.at[rho, h, b1, 1], RD.at[rho, h, 0, 1], self.sp)
            self.put(9, R1B.at[rho, h, b3, 0], RD.at[rho, h, 1, 0], self.sm)

        def step4(self):
            rho, h, b = self.rho, self.h, self.b
            b1, b3 = m4(b + 1), m4(b + 3)
            self.get(6, RC.at[rho, h, 0])
            CS2[rho, h, 0] = (R1[rho, h, b1, 0] + RC[rho, h, 0].astype(F32)).astype(BF)
            self.put(10, CS2.at[rho, h, 0], RD.at[rho, h, 0, 0], self.sp)
            self.get(7, RC.at[rho, h, 1])
            CS2[rho, h, 1] = (R1[rho, h, b3, 1] + RC[rho, h, 1].astype(F32)).astype(BF)
            self.put(11, CS2.at[rho, h, 1], RD.at[rho, h, 1, 1], self.sm)

        def step5(self):
            rho, h, b = self.rho, self.h, self.b
            self.get(8, RD.at[rho, h, 0, 1])
            self.get(9, RD.at[rho, h, 1, 0])
            self.get(10, RD.at[rho, h, 0, 0])
            self.get(11, RD.at[rho, h, 1, 1])
            s = R1[rho, h, b] + RD[rho, h, 0].astype(F32) + RD[rho, h, 1].astype(F32)
            if rho == 0:
                R2[h] = s
            else:
                ZS[h] = s.astype(BF)
                send(lambda: rcopy(ZS.at[h], ZR.at[h], zss.at[h], zsr.at[h], zz))

        def out(self):
            h = self.h
            arrive(ZR.at[h], zss.at[h], zsr.at[h])
            OUT[:, h * 768:(h + 1) * 768] = (R2[h] + ZR[h].astype(F32)).astype(BF).reshape(32, 768)

    sc = [[Scatter(rho, h) for h in range(2)] for rho in range(2)]

    def mask_weights():
        @pl.loop(0, 12)
        def _(i):
            rows = pl.ds(pl.multiple_of(i * 128, 128), 128)
            for j in range(6):
                cols = slice(j * 128, (j + 1) * 128)
                m = upp[i, j].astype(F32)
                U[rows, cols] = (U[rows, cols].astype(F32) * m).astype(BF)

        @pl.loop(0, 12)
        def _(i):
            cols = pl.ds(pl.multiple_of(i * 128, 128), 128)
            for j in range(6):
                rows = slice(j * 128, (j + 1) * 128)
                m = dnp[j, i].astype(F32)
                D[rows, cols] = (D[rows, cols].astype(F32) * m).astype(BF)

    factor = 1.0 / 32.0

    def up_grads(lo, hi):
        @pl.loop(lo, hi)
        def _(n):
            cols = pl.ds(pl.multiple_of(n * 256, 256), 256)
            t = T[:, :, :, :, :, cols].reshape(1024, 256)
            for f in range(3):
                dh = AD[:, f, :, :, 1].reshape(1024, 256)
                res = lax.dot_general(t, dh, TN, preferred_element_type=F32)
                for bi in range(2):
                    for bj in range(2):
                        m = upp[n * 2 + bi, f * 2 + bj].astype(F32) * factor
                        UG[
                            pl.ds(pl.multiple_of(n * 256 + bi * 128, 128), 128),
                            f * 256 + bj * 128:f * 256 + (bj + 1) * 128,
                        ] = (res[bi * 128:(bi + 1) * 128, bj * 128:(bj + 1) * 128] * m).astype(BF)

    def down_grads(lo, hi):
        @pl.loop(lo, hi)
        def _(n):
            cols = pl.ds(pl.multiple_of(n * 256, 256), 256)
            g = G[:, :, :, :, :, cols].reshape(1024, 256)
            for f in range(3):
                ac = AD[:, f, :, :, 0].reshape(1024, 256)
                res = lax.dot_general(ac, g, TN, preferred_element_type=F32)
                for bi in range(2):
                    for bj in range(2):
                        m = dnp[f * 2 + bi, n * 2 + bj].astype(F32) * factor
                        DG[
                            f * 256 + bi * 128:f * 256 + (bi + 1) * 128,
                            pl.ds(pl.multiple_of(n * 256 + bj * 128, 128), 128),
                        ] = (res[bi * 128:(bi + 1) * 128, bj * 128:(bj + 1) * 128] * m).astype(BF)

    gt0.start()
    gg0.start()
    across(T, 0)
    across(G, 1)
    locals_[2].wait()
    locals_[3].wait()
    mask_weights()
    gt0.step2()
    gg0.step2()
    gt0.step3()
    gg0.step3()
    gt0.step4a()
    gg0.step4a()
    gt0.step4b()
    gg0.step4b()
    across_wait(T, 0)
    gt1.start()
    across_wait(G, 1)
    gg1.start()
    gt0.finish()
    gg0.finish()

    def burst(rho, extra):
        i0 = rho * 3
        stages = [row_a, row_b, lambda i: row_c(i, 2), lambda i: row_c(i, 1), row_d,
                  lambda i: row_e(i, 1), lambda i: row_e(i, 2), lambda i: row_e(i, 3), row_f]
        for t in range(11):
            order = range(3)
            for f in order:
                s = t - f
                if 0 <= s < 9:
                    stages[s](i0 + f)
            for fn in extra.get(t, ()):
                fn()

    burst(0, {
        1: (gt1.step2, gg1.step2),
        3: (gt1.step3, gg1.step3),
        5: (gt1.step4a, gg1.step4a),
        7: (gt1.step4b, gg1.step4b),
    })
    gt1.finish()
    gg1.finish()

    def both(rho, name):
        def run():
            for h in range(2):
                getattr(sc[rho][h], name)()
        return run

    def ig0():
        for h in range(2):
            ig_matmul(0, h)
            sc[0][h].start()

    burst(1, {
        2: (ig0,),
        4: (both(0, "step2"),),
        5: (both(0, "step3"),),
        7: (both(0, "step4"),),
        8: (both(0, "step5"),),
    })
    for h in range(2):
        ig_matmul(1, h)
        sc[1][h].start()
    up_grads(0, 3)
    both(1, "step2")()
    up_grads(3, 6)
    both(1, "step3")()
    down_grads(0, 2)
    both(1, "step4")()
    down_grads(2, 4)
    both(1, "step5")()
    up_copy = pltpu.make_async_copy(UG, ug_out, lsem.at[0])
    up_copy.start()
    down_grads(4, 6)
    dn_copy = pltpu.make_async_copy(DG, dg_out, lsem.at[1])
    dn_copy.start()
    for h in range(2):
        sc[0][h].out()
    ig_copy = pltpu.make_async_copy(OUT, ig_out, lsem.at[2])
    ig_copy.start()

    for cond, make in pending:
        if cond is None:
            make().wait_send()
        else:
            @pl.when(cond)
            def _():
                make().wait_send()
    up_copy.wait()
    dn_copy.wait()
    ig_copy.wait()


def on_device(tokens, up_weight, down_weight, cotangent, up_pattern, down_pattern):
    any_ = pl.BlockSpec(memory_space=pl.ANY)
    smem = pl.BlockSpec(memory_space=pltpu.SMEM)
    dma = pltpu.SemaphoreType.DMA
    V = pltpu.VMEM
    return pl.pallas_call(
        kernel,
        out_shape=(
            jax.ShapeDtypeStruct((32, 1536), BF),
            jax.ShapeDtypeStruct((1536, 768), BF),
            jax.ShapeDtypeStruct((768, 1536), BF),
        ),
        in_specs=[any_, any_, any_, any_, smem, smem],
        out_specs=(any_, any_, any_),
        scratch_shapes=[
            V((2, 4, 2, 4, 16, 1536), BF),
            V((2, 4, 2, 4, 16, 1536), BF),
            V((1536, 768), BF),
            V((768, 1536), BF),
            V((6, 2, 4, 2, 4, 16, 256), F32),
            V((6, 2, 4, 4, 16, 256), BF),
            V((6, 2, 4, 4, 16, 256), BF),
            V((6, 2, 3, 2, 4, 16, 256), BF),
            V((6, 2, 3, 2, 4, 16, 256), BF),
            V((2, 3, 4, 2, 2, 4, 16, 256), BF),
            V((2, 2, 4, 4, 2, 16, 768), BF),
            V((2, 2, 2, 2, 2, 16, 768), BF),
            V((2, 2, 2, 4, 2, 16, 768), BF),
            V((2, 2, 2, 2, 2, 16, 768), BF),
            V((2, 2, 4, 2, 16, 768), F32),
            V((2, 2, 4, 2, 16, 768), BF),
            V((2, 2, 2, 16, 768), BF),
            V((2, 2, 2, 2, 16, 768), BF),
            V((2, 2, 2, 16, 768), BF),
            V((2, 2, 16, 768), F32),
            V((2, 2, 16, 768), BF),
            V((2, 2, 16, 768), BF),
            V((1536, 768), BF),
            V((768, 1536), BF),
            V((32, 1536), BF),
            dma((4,)),
            dma((2, 2, 16)), dma((2, 2, 16)),
            dma((2,)), dma((2,)),
            dma((6,)), dma((6,)),
            dma((6, 2, 3)), dma((6, 2, 3)),
            dma((6, 2, 3)), dma((6, 2, 3)),
            dma((6, 7)), dma((6, 7)),
            dma((2, 2, 12)), dma((2, 2, 12)),
            dma((2,)), dma((2,)),
        ],
        compiler_params=pltpu.CompilerParams(
            collective_id=0, has_side_effects=True, vmem_limit_bytes=62 * 1024 * 1024
        ),
    )(
        tokens.reshape(2, 16, 1536),
        up_weight,
        down_weight,
        cotangent.reshape(2, 16, 1536),
        up_pattern,
        down_pattern,
    )


def solution(mesh):
    return jax.shard_map(
        on_device,
        mesh=mesh,
        in_specs=(
            P("col", "row"),
            P("row", "col"),
            P("col", "row"),
            P("col", "row"),
            P("row", "col"),
            P("col", "row"),
        ),
        out_specs=(P("col", "row"), P("row", "col"), P("col", "row")),
        check_vma=False,
    )
```

```python
import jax
import jax.numpy as jnp
from jax import lax
from jax.experimental import pallas as pl
from jax.experimental.pallas import tpu as pltpu
from jax.sharding import PartitionSpec as P

MESH = pl.DeviceIdType.MESH
HALF_ROOT = 0.7071067811865476
INV_ROOT_TAU = 0.3989422804014327
BF = jnp.bfloat16
F32 = jnp.float32
NT = (((1,), (1,)), ((), ()))
TN = (((0,), (0,)), ((), ()))

ORDER = (
    0, 11, 44, 45, 46, 1, 12, 2, 13, 3, 14, 17, 6, 4, 15, 5, 16, 49, 57, 18, 7, 47, 22, 48,
    33, 23, 34, 50, 58, 51, 54, 19, 8, 9, 20, 65, 73, 59, 62, 81, 89, 66, 52, 55, 74, 82, 90, 35,
    24, 25, 36, 60, 63, 67, 70, 53, 56, 21, 10, 97, 75, 78, 105, 61, 64, 114, 83, 86, 98, 91, 94, 68,
    71, 37, 200, 26, 27, 38, 106, 192, 28, 39, 76, 79, 115, 84, 87, 201, 29, 40, 102, 99, 193, 69, 72, 92,
    95, 169, 110, 107, 77, 80, 137, 30, 31, 41, 42, 208, 117, 216, 88, 202, 145, 205, 122, 85, 224, 103, 100, 194,
    154, 93, 197, 96, 232, 111, 121, 108, 209, 172, 217, 225, 119, 140, 32, 240, 43, 203, 206, 233, 123, 248, 104, 101,
    195, 198, 148, 155, 124, 112, 109, 174, 210, 241, 213, 249, 142, 218, 204, 207, 221, 125, 226, 150, 130, 196, 199, 229,
    157, 113, 234, 126, 138, 176, 237, 211, 129, 242, 214, 146, 144, 245, 219, 127, 153, 250, 222, 162, 152, 253, 227, 159,
    161, 131, 230, 170, 128, 116, 235, 212, 312, 139, 238, 257, 215, 132, 243, 220, 280, 147, 246, 223, 156, 251, 228, 288,
    163, 254, 231, 164, 133, 265, 236, 264, 297, 171, 118, 239, 315, 141, 244, 272, 281, 258, 134, 247, 283, 149, 252, 256,
    289, 158, 255, 291, 165, 135, 266, 296, 273, 166, 120, 267, 173, 143, 298, 304, 305, 317, 136, 275, 260, 151, 282, 313,
    160, 167, 285, 290, 259, 168, 268, 299, 175, 177, 178, 269, 274, 293, 319, 262, 306, 300, 284, 307, 179, 185, 277, 314,
    186, 292, 180, 287, 261, 276, 187, 271, 301, 270, 302, 295, 308, 309, 286, 181, 279, 316, 294, 188, 263, 278, 303, 310,
    311, 318, 320, 321, 322, 328, 329, 182, 189, 335, 337, 323, 339, 330, 341, 324, 190, 331, 343, 183, 345, 336, 325, 191,
    332, 338, 184, 340, 326, 333, 342, 327, 334, 344, 346, 347, 348,
)


def kernel(
    tok, upw, dnw, cot, upp, dnp, ig_out, ug_out, dg_out,
    T, G, U, D, DT, PS, XS, XR, RSS, RSR, AD, IG, RA, RB, CS, R1, R1B, RC, RD, CS2, R2, ZS, ZR, UG, DG, OUT,
    lsem, ags, agr, zxs, zxr, xss, xr, rss, rsr, ads, adr, acs, acr, igs, igr, zss, zsr,
):
    r = lax.axis_index("row")
    q = lax.axis_index("col")
    zl, c = r // 2, lax.rem(r, 2)
    zh = q // 16
    y = lax.rem(q // 4, 4)
    x = lax.rem(q, 4)
    oc = 1 - c

    def m4(v):
        return lax.rem(v, 4)

    xp = (r, zh * 16 + y * 4 + m4(x + 1))
    xm = (r, zh * 16 + y * 4 + m4(x + 3))
    yp = (r, zh * 16 + m4(y + 1) * 4 + x)
    ym = (r, zh * 16 + m4(y + 3) * 4 + x)
    zz = (r, (1 - zh) * 16 + y * 4 + x)
    co = (zl * 2 + oc, q)
    zp = (m4(zl + 1) * 2 + c, q)
    zm = (m4(zl + 3) * 2 + c, q)

    o0 = m4(x + y)
    locals_ = [
        pltpu.make_async_copy(tok, T.at[0, o0, :, y], lsem.at[0]),
        pltpu.make_async_copy(cot, G.at[0, o0, :, y], lsem.at[1]),
        pltpu.make_async_copy(upw, U, lsem.at[2]),
        pltpu.make_async_copy(dnw, D, lsem.at[3]),
    ]
    for d in locals_:
        d.start()

    barrier = pltpu.get_barrier_semaphore()
    for dev in (xp, xm, yp, ym, zz, co, zp, zm):
        pl.semaphore_signal(barrier, inc=1, device_id=dev, device_id_type=MESH)
    locals_[0].wait()
    locals_[1].wait()
    pl.semaphore_wait(barrier, 8)

    pending = []

    def rcopy(src, dst, ss, rs, dev):
        return pltpu.make_async_remote_copy(
            src_ref=src, dst_ref=dst, send_sem=ss, recv_sem=rs, device_id=dev, device_id_type=MESH
        )

    def send(make, cond=None):
        if cond is None:
            make().start()
        else:
            @pl.when(cond)
            def _():
                make().start()

    def arrive(ref, rs):
        rcopy(ref, ref, xss, rs, co).wait_recv()

    def sent(ref, ss, cond=None):
        pending.append((cond, lambda: rcopy(ref, ref, ss, zsr.at[0], co)))

    class Gather:
        def __init__(self, A, arr, rho):
            self.A, self.arr, self.rho = A, arr, rho
            self.fp, self.fm, self.sp, self.sm = (xp, xm, yp, ym) if arr == 0 else (yp, ym, xp, xm)
            sent(A.at[rho, 0, :, 0:3], ags.at[arr, rho, 0])
            sent(A.at[rho, 0:3], ags.at[arr, rho, 1])

        def ref(self, da, db, h=None):
            da, db = da % 4, db % 4
            xx, yy = (m4(x + da), m4(y + db)) if self.arr == 0 else (m4(x + db), m4(y + da))
            o = m4(xx + yy)
            if h is None:
                return self.A.at[self.rho, o, :, yy]
            return self.A.at[self.rho, o, h, yy]

        slots = {0: 0, 1: 1, 4: 2, 7: 2, 2: 3, 6: 4, 8: 5, 11: 6, 3: 7, 5: 7, 9: 7, 10: 7, 12: 8, 13: 8, 14: 8, 15: 8}

        def put(self, k, ref, dev):
            ss = ags.at[self.arr, self.rho, 0 if k in (0, 1, 4, 7) else 1]
            rs = agr.at[self.arr, self.rho, self.slots[k]]
            send(lambda: rcopy(ref, ref, ss, rs, dev))

        def get(self, k, ref):
            arrive(ref, agr.at[self.arr, self.rho, self.slots[k]])

        def start_a(self):
            own = self.ref(0, 0)
            self.put(0, own, self.fp)
            self.put(1, own, self.fm)

        def start_b(self):
            own = self.ref(0, 0)
            self.put(2, own, self.sp)
            self.put(3, own, self.sm)

        def step2a(self):
            self.get(0, self.ref(-1, 0))
            self.put(4, self.ref(-1, 0, 0), self.fp)
            self.get(1, self.ref(1, 0))
            self.put(7, self.ref(1, 0, 1), self.fm)

        def step2b(self):
            self.put(5, self.ref(-1, 0), self.sp)
            self.put(6, self.ref(-1, 0), self.sm)
            self.put(8, self.ref(1, 0), self.sp)
            self.put(9, self.ref(1, 0), self.sm)

        def step3(self):
            self.get(4, self.ref(2, 0))
            self.put(10, self.ref(2, 0), self.sp)
            self.put(11, self.ref(2, 0), self.sm)

        def step4a(self):
            self.get(2, self.ref(0, -1))
            self.put(12, self.ref(0, -1), self.sp)

        def step4b(self):
            self.get(6, self.ref(-1, 1))
            self.put(13, self.ref(-1, 1), self.sm)

        def step4c(self):
            self.get(8, self.ref(1, -1))
            self.put(14, self.ref(1, -1), self.sp)

        def step4d(self):
            self.get(11, self.ref(2, 1))
            self.put(15, self.ref(2, 1), self.sm)

        def near(self):
            self.get(3, self.A.at[self.rho, 0])

        def far(self):
            self.get(12, self.A.at[self.rho, 0])

    gt0, gg0 = Gather(T, 0, 0), Gather(G, 1, 0)
    gt1, gg1 = Gather(T, 0, 1), Gather(G, 1, 1)

    def across(A, k):
        src, dst = A.at[0, o0, :, y], A.at[1, o0, :, y]
        sent(src, zxs.at[k])
        send(lambda: rcopy(src, dst, zxs.at[k], zxr.at[k], zz))

    def across_wait(A, k):
        arrive(A.at[1, o0, :, y], zxr.at[k])

    shift = (0, 3, 1, 2)

    def slot(do):
        return m4(x + y + do)

    def shard_row(arr, g, do):
        if arr == 0:
            return m4(y + shift[g])
        return m4(slot(do) + 4 - m4(x + shift[g]))

    def row_a(rho, arr, g):
        A = G if arr else T
        t = jnp.concatenate([A[rho, slot(o), :, shard_row(arr, g, o)].reshape(32, 1536) for o in range(4)], axis=0)
        if arr == 0:
            p = jnp.dot(t, U[...], preferred_element_type=F32)
        else:
            p = jnp.dot(t, DT[...], preferred_element_type=F32)
        p = p.reshape(4, 2, 16, 768)
        for o in range(4):
            PS[rho, arr, slot(o), :, shard_row(arr, g, o)] = p[o]
        for o in range(4):
            XS[rho, arr, g, o] = PS[rho, arr, slot(o), oc, shard_row(arr, g, o)].astype(BF)
        send(lambda: rcopy(XS.at[rho, arr, g], XR.at[rho, arr, g], xss, xr.at[rho, arr, g], co))

    def block_of(way, j):
        return 2 + j if way == 0 else j

    def rs_pass(rho, arr, g, way):
        dev = zp if way == 0 else zm
        k = (rho, arr, g, way)
        return lambda: rcopy(RSS.at[k], RSR.at[k], rss.at[way], rsr.at[k], dev)

    def rs_arrive(rho, arr, g, way):
        k = (rho, arr, g, way)
        arrive(RSR.at[k], rsr.at[k])

    def row_b(rho, arr, g):
        arrive(XR.at[rho, arr, g], xr.at[rho, arr, g])
        for way, first in ((0, 0), (1, 3)):
            make = rs_pass(rho, arr, g, way)
            cond = zl == first
            for j in range(2):
                o = block_of(way, j)
                yy = shard_row(arr, g, o)
                s = PS[rho, arr, slot(o), c, yy] + XR[rho, arr, g, o].astype(F32)
                PS[rho, arr, slot(o), c, yy] = s

                @pl.when(cond)
                def _():
                    RSS[rho, arr, g, way, j] = s.astype(BF)

            send(make, cond)

    def row_c(rho, arr, g, hop, way):
        make = rs_pass(rho, arr, g, way)

        @pl.when(zl == (hop if way == 0 else 3 - hop))
        def _():
            rs_arrive(rho, arr, g, way)
            for j in range(2):
                o = block_of(way, j)
                s = PS[rho, arr, slot(o), c, shard_row(arr, g, o)] + RSR[rho, arr, g, way, j].astype(F32)
                RSS[rho, arr, g, way, j] = s.astype(BF)
            make().start()

    def row_sum(rho, arr, g, way):
        @pl.when(zl == (3 if way == 0 else 0))
        def _():
            rs_arrive(rho, arr, g, way)
            for j in range(2):
                o = block_of(way, j)
                yy = shard_row(arr, g, o)
                PS[rho, arr, slot(o), c, yy] = PS[rho, arr, slot(o), c, yy] + RSR[rho, arr, g, way, j].astype(F32)

    sent(XS, xss)
    sent(RSS.at[:, :, :, 0], rss.at[0], zl <= 2)
    sent(RSS.at[:, :, :, 1], rss.at[1], zl >= 1)
    sent(AD.at[:, 0:2, c], ads.at[0], zl <= 2)
    sent(AD.at[:, 2:4, c], ads.at[1], zl >= 1)
    sent(AD.at[:, :, c], acs)

    def ad_block(rho, o, yy, core):
        return AD.at[rho, o, core, yy]

    def ad_line(rho, way, k):
        dev = zp if way == 0 else zm
        ref = ad_block(rho, slot(block_of(1 - way, k // 4)), m4(y + k % 4), c)
        return lambda: rcopy(ref, ref, ads.at[way], adr.at[rho, way, k], dev)

    def ad_core(rho, o, yy):
        ref = ad_block(rho, o, yy, c)
        return lambda: rcopy(ref, ref, acs, acr.at[rho], co)

    def row_d(rho, k, way):
        o, yy = slot(block_of(way, k // 4)), m4(y + k % 4)
        line, core = ad_line(rho, 1 - way, k), ad_core(rho, o, yy)

        @pl.when(zl == (3 if way == 0 else 0))
        def _():
            pre = PS[rho, 0, o, c, yy]
            dact = PS[rho, 1, o, c, yy]
            cdf = 0.5 * (1.0 + lax.erf(pre * HALF_ROOT))
            dens = jnp.exp(-0.5 * pre * pre) * INV_ROOT_TAU
            AD[rho, o, c, yy, 0] = (pre * cdf).astype(BF)
            AD[rho, o, c, yy, 1] = (dact * (cdf + pre * dens)).astype(BF)
            line().start()
            core().start()

    def row_e(rho, k, hop, way):
        o, yy = slot(block_of(1 - way, k // 4)), m4(y + k % 4)
        line, core = ad_line(rho, way, k), ad_core(rho, o, yy)

        @pl.when(zl == (hop if way == 0 else 3 - hop))
        def _():
            arrive(ad_block(rho, o, yy, c), adr.at[rho, way, k])
            if hop < 3:
                line().start()
            core().start()

    def row_f(rho):
        arrive(AD.at[rho, :, oc], acr.at[rho])

    def ig_matmul(rho, h):
        @pl.loop(0, 3)
        def _(n):
            rows = pl.ds(pl.multiple_of(h * 768 + n * 256, 256), 256)
            cols = pl.ds(pl.multiple_of(n * 256, 256), 256)
            for o in range(0, 4, 2):
                dh = AD[rho, o:o + 2, :, :, 1].reshape(256, 768)
                acc = lax.dot_general(dh, U[rows, :], NT, preferred_element_type=F32)
                acc = acc.astype(BF).reshape(2, 2, 4, 16, 256)
                for oo in range(2):
                    for yy in range(4):
                        xx = (o + oo - yy) % 4
                        a, b = (yy, xx) if h == 0 else (xx, yy)
                        IG[rho, h, a, b, :, :, cols] = acc[oo, :, yy]

    class Scatter:
        def __init__(self, rho, h):
            self.rho, self.h = rho, h
            self.fp, self.fm, self.sp, self.sm = (yp, ym, xp, xm) if h == 0 else (xp, xm, yp, ym)
            self.a, self.b = (y, x) if h == 0 else (x, y)

            sent(IG.at[rho, h, 0:3], igs.at[rho, h, 0])
            sent(IG.at[rho, h, 0, 0:3], igs.at[rho, h, 1])

        slots = {0: 0, 1: 0, 2: 1, 3: 1, 4: 1, 5: 1, 6: 2, 7: 2, 8: 3, 9: 3, 10: 3, 11: 3}

        def put(self, k, src, dst, dev):
            ss, rs = igs.at[self.rho, self.h, 0 if k < 6 else 1], igr.at[self.rho, self.h, self.slots[k]]
            send(lambda: rcopy(src, dst, ss, rs, dev))

        def get(self, k, ref):
            arrive(ref, igr.at[self.rho, self.h, self.slots[k]])

        def start(self):
            i = (self.rho, self.h)
            a = self.a
            a2 = m4(a + 2)
            self.put(0, IG.at[i[0], i[1], a2, 0:2], RA.at[i[0], i[1], 0], self.fp)
            self.put(1, IG.at[i[0], i[1], a2, 2:4], RA.at[i[0], i[1], 1], self.fm)

        def start_b(self):
            i = (self.rho, self.h)
            a1, a3 = m4(self.a + 1), m4(self.a + 3)
            self.put(2, IG.at[i[0], i[1], a1, 2:4], RB.at[i[0], i[1], 0, 2:4], self.fp)
            self.put(3, IG.at[i[0], i[1], a3, 0:2], RB.at[i[0], i[1], 1, 0:2], self.fm)

        def step2(self):
            rho, h, a = self.rho, self.h, self.a
            a1, a3 = m4(a + 1), m4(a + 3)
            self.get(0, RA.at[rho, h])
            CS[rho, h, 0] = (IG[rho, h, a1, 0:2].astype(F32) + RA[rho, h, 0].astype(F32)).astype(BF)
            self.put(4, CS.at[rho, h, 0], RB.at[rho, h, 0, 0:2], self.fp)
            CS[rho, h, 1] = (IG[rho, h, a3, 2:4].astype(F32) + RA[rho, h, 1].astype(F32)).astype(BF)
            self.put(5, CS.at[rho, h, 1], RB.at[rho, h, 1, 2:4], self.fm)

        def step3(self):
            rho, h, a, b = self.rho, self.h, self.a, self.b
            self.get(2, RB.at[rho, h])
            for k in range(4):
                s = IG[rho, h, a, k].astype(F32) + RB[rho, h, 0, k].astype(F32) + RB[rho, h, 1, k].astype(F32)
                R1[rho, h, k] = s
                R1B[rho, h, k] = s.astype(BF)
            b1, b2, b3 = m4(b + 1), m4(b + 2), m4(b + 3)
            self.put(6, R1B.at[rho, h, b2, 0], RC.at[rho, h, 0], self.sp)
            self.put(7, R1B.at[rho, h, b2, 1], RC.at[rho, h, 1], self.sm)
            self.put(8, R1B.at[rho, h, b1, 1], RD.at[rho, h, 0, 1], self.sp)
            self.put(9, R1B.at[rho, h, b3, 0], RD.at[rho, h, 1, 0], self.sm)

        def step4(self):
            rho, h, b = self.rho, self.h, self.b
            b1, b3 = m4(b + 1), m4(b + 3)
            self.get(6, RC.at[rho, h])
            CS2[rho, h, 0] = (R1[rho, h, b1, 0] + RC[rho, h, 0].astype(F32)).astype(BF)
            self.put(10, CS2.at[rho, h, 0], RD.at[rho, h, 0, 0], self.sp)
            CS2[rho, h, 1] = (R1[rho, h, b3, 1] + RC[rho, h, 1].astype(F32)).astype(BF)
            self.put(11, CS2.at[rho, h, 1], RD.at[rho, h, 1, 1], self.sm)

        def step5(self):
            rho, h, b = self.rho, self.h, self.b
            self.get(8, RD.at[rho, h])
            s = R1[rho, h, b] + RD[rho, h, 0].astype(F32) + RD[rho, h, 1].astype(F32)
            if rho == 0:
                R2[h] = s
            else:
                ZS[h] = s.astype(BF)
                sent(ZS.at[h], zss.at[h])
                send(lambda: rcopy(ZS.at[h], ZR.at[h], zss.at[h], zsr.at[h], zz))

        def out(self):
            h = self.h
            arrive(ZR.at[h], zsr.at[h])
            OUT[:, h * 768:(h + 1) * 768] = (R2[h] + ZR[h].astype(F32)).astype(BF).reshape(32, 768)

    sc = [[Scatter(rho, h) for h in range(2)] for rho in range(2)]

    def mask_weights():
        @pl.loop(0, 12)
        def _(i):
            rows = pl.ds(pl.multiple_of(i * 128, 128), 128)
            for j in range(6):
                cols = slice(j * 128, (j + 1) * 128)
                m = upp[j, i].astype(F32)
                U[rows, cols] = (U[rows, cols].astype(F32) * m).astype(BF)

        @pl.loop(0, 12)
        def _(i):
            cols = pl.ds(pl.multiple_of(i * 128, 128), 128)
            for j in range(6):
                rows = slice(j * 128, (j + 1) * 128)
                m = dnp[j, i].astype(F32)
                DT[cols, rows] = (D[rows, cols].astype(F32) * m).T.astype(BF)

    factor = 1.0 / 32.0

    def up_grads(lo, hi):
        @pl.loop(lo, hi)
        def _(n):
            cols = pl.ds(pl.multiple_of(n * 256, 256), 256)
            t = T[:, :, :, :, :, cols].reshape(1024, 256)
            for f in range(3):
                dh = AD[:, :, :, :, 1, :, f * 256:(f + 1) * 256].reshape(1024, 256)
                res = lax.dot_general(t, dh, TN, preferred_element_type=F32)
                for bi in range(2):
                    for bj in range(2):
                        m = upp[f * 2 + bj, n * 2 + bi].astype(F32) * factor
                        UG[
                            pl.ds(pl.multiple_of(n * 256 + bi * 128, 128), 128),
                            f * 256 + bj * 128:f * 256 + (bj + 1) * 128,
                        ] = (res[bi * 128:(bi + 1) * 128, bj * 128:(bj + 1) * 128] * m).astype(BF)

    def down_grads(lo, hi):
        @pl.loop(lo, hi)
        def _(n):
            cols = pl.ds(pl.multiple_of(n * 256, 256), 256)
            g = G[:, :, :, :, :, cols].reshape(1024, 256)
            for f in range(3):
                ac = AD[:, :, :, :, 0, :, f * 256:(f + 1) * 256].reshape(1024, 256)
                res = lax.dot_general(ac, g, TN, preferred_element_type=F32)
                for bi in range(2):
                    for bj in range(2):
                        m = dnp[f * 2 + bi, n * 2 + bj].astype(F32) * factor
                        DG[
                            f * 256 + bi * 128:f * 256 + (bi + 1) * 128,
                            pl.ds(pl.multiple_of(n * 256 + bj * 128, 128), 128),
                        ] = (res[bi * 128:(bi + 1) * 128, bj * 128:(bj + 1) * 128] * m).astype(BF)

    def put_up(lo, hi):
        up_grads(lo, hi)
        rows = slice(lo * 256, hi * 256)
        pltpu.make_async_copy(UG.at[rows], ug_out.at[rows], lsem.at[4]).start()

    def put_down(lo, hi):
        down_grads(lo, hi)
        cols = slice(lo * 256, hi * 256)
        pltpu.make_async_copy(DG.at[:, cols], dg_out.at[:, cols], lsem.at[5]).start()

    steps = {}

    def at(name, fn, *args):
        steps[name] = (fn, args)

    def weights():
        locals_[2].wait()
        locals_[3].wait()
        mask_weights()

    for name, gt in (("g0t", gt0), ("g0g", gg0), ("g1t", gt1), ("g1g", gg1)):
        for step in ("start_a", "start_b", "step2a", "step2b", "step3", "step4a", "step4b", "step4c", "step4d", "near", "far"):
            at(name + "_" + step, getattr(gt, step))
    at("acrossT", across, T, 0)
    at("acrossG", across, G, 1)
    at("weights", weights)
    at("awaitT", across_wait, T, 0)
    at("awaitG", across_wait, G, 1)
    for rho in range(2):
        for g in range(4):
            for arr in range(2):
                n = "%d%d%d" % (rho, arr, g)
                at("a" + n, row_a, rho, arr, g)
                at("b" + n, row_b, rho, arr, g)
                for way, w in enumerate("rl"):
                    at("c1" + w + n, row_c, rho, arr, g, 1, way)
                    at("c2" + w + n, row_c, rho, arr, g, 2, way)
                    at("s" + w + n, row_sum, rho, arr, g, way)
        for k in range(8):
            n = "%d%d" % (rho, k)
            at("dr" + n, row_d, rho, k, 0)
            at("dl" + n, row_d, rho, k, 1)
            for hop in (1, 2, 3):
                at("e%dl" % hop + n, row_e, rho, k, hop, 0)
                at("e%dr" % hop + n, row_e, rho, k, hop, 1)
        at("f%d" % rho, row_f, rho)
        for h in range(2):
            n = "%d%d" % (rho, h)
            at("ig" + n, ig_matmul, rho, h)
            at("st" + n, sc[rho][h].start)
            at("sb" + n, sc[rho][h].start_b)
            for k in (2, 3, 4, 5):
                at("s%d" % k + n, getattr(sc[rho][h], "step%d" % k))
    for k in range(6):
        at("up%d" % k, put_up, k, k + 1)
        at("dn%d" % k, put_down, k, k + 1)
    at("out0", sc[0][0].out)
    at("out1", sc[0][1].out)

    names = list(steps)
    assert sorted(ORDER) == list(range(len(names)))
    for name in (names[k] for k in ORDER):
        fn, args = steps[name]
        with jax.named_scope(name):
            fn(*args)

    ig_copy = pltpu.make_async_copy(OUT, ig_out, lsem.at[0])
    ig_copy.start()

    with jax.named_scope("drain"):
        for cond, make in pending:
            if cond is None:
                make().wait_send()
            else:
                @pl.when(cond)
                def _():
                    make().wait_send()
    pltpu.make_async_copy(UG, ug_out, lsem.at[4]).wait()
    pltpu.make_async_copy(DG, dg_out, lsem.at[5]).wait()
    ig_copy.wait()


def on_device(tokens, up_weight, down_weight, cotangent, up_pattern, down_pattern):
    any_ = pl.BlockSpec(memory_space=pl.ANY)
    smem = pl.BlockSpec(memory_space=pltpu.SMEM)
    dma = pltpu.SemaphoreType.DMA
    V = pltpu.VMEM
    return pl.pallas_call(
        kernel,
        out_shape=(
            jax.ShapeDtypeStruct((32, 1536), BF),
            jax.ShapeDtypeStruct((1536, 768), BF),
            jax.ShapeDtypeStruct((768, 1536), BF),
        ),
        in_specs=[any_, any_, any_, any_, smem, smem],
        out_specs=(any_, any_, any_),
        scratch_shapes=[
            V((2, 4, 2, 4, 16, 1536), BF),
            V((2, 4, 2, 4, 16, 1536), BF),
            V((1536, 768), BF),
            V((768, 1536), BF),
            V((1536, 768), BF),
            V((2, 2, 4, 2, 4, 16, 768), F32),
            V((2, 2, 4, 4, 16, 768), BF),
            V((2, 2, 4, 4, 16, 768), BF),
            V((2, 2, 4, 2, 2, 16, 768), BF),
            V((2, 2, 4, 2, 2, 16, 768), BF),
            V((2, 4, 2, 4, 2, 16, 768), BF),
            V((2, 2, 4, 4, 2, 16, 768), BF),
            V((2, 2, 2, 2, 2, 16, 768), BF),
            V((2, 2, 2, 4, 2, 16, 768), BF),
            V((2, 2, 2, 2, 2, 16, 768), BF),
            V((2, 2, 4, 2, 16, 768), F32),
            V((2, 2, 4, 2, 16, 768), BF),
            V((2, 2, 2, 16, 768), BF),
            V((2, 2, 2, 2, 16, 768), BF),
            V((2, 2, 2, 16, 768), BF),
            V((2, 2, 16, 768), F32),
            V((2, 2, 16, 768), BF),
            V((2, 2, 16, 768), BF),
            V((1536, 768), BF),
            V((768, 1536), BF),
            V((32, 1536), BF),
            dma((7,)),
            dma((2, 2, 2)), dma((2, 2, 9)),
            dma((2,)), dma((2,)),
            dma, dma((2, 2, 4)),
            dma((2,)), dma((2, 2, 4, 2)),
            dma((2,)), dma((2, 2, 8)),
            dma, dma((2,)),
            dma((2, 2, 2)), dma((2, 2, 4)),
            dma((2,)), dma((2,)),
        ],
        compiler_params=pltpu.CompilerParams(
            collective_id=0, has_side_effects=True, vmem_limit_bytes=62 * 1024 * 1024
        ),
    )(
        tokens.reshape(2, 16, 1536),
        up_weight,
        down_weight,
        cotangent.reshape(2, 16, 1536),
        up_pattern.T,
        down_pattern,
    )


def solution(mesh):
    return jax.shard_map(
        on_device,
        mesh=mesh,
        in_specs=(
            P("col", "row"),
            P("row", "col"),
            P("col", "row"),
            P("col", "row"),
            P("row", "col"),
            P("col", "row"),
        ),
        out_specs=(P("col", "row"), P("row", "col"), P("col", "row")),
        check_vma=False,
    )
```

```python
import jax
import jax.numpy as jnp
from jax import lax
from jax.experimental import pallas as pl
from jax.experimental.pallas import tpu as pltpu
from jax.sharding import PartitionSpec as P

MESH = pl.DeviceIdType.MESH
HALF_ROOT = 0.7071067811865476
INV_ROOT_TAU = 0.3989422804014327
BF = jnp.bfloat16
F32 = jnp.float32
NT = (((1,), (1,)), ((), ()))
TN = (((0,), (0,)), ((), ()))

ORDER = (
    0, 11, 44, 45, 46, 1, 12, 2, 13, 3, 14, 17, 6, 4, 15, 5, 16, 49, 57, 18, 7, 47, 22, 48,
    33, 23, 34, 50, 58, 51, 54, 19, 8, 9, 20, 65, 73, 59, 62, 81, 89, 66, 52, 55, 74, 82, 90, 35,
    24, 25, 36, 60, 63, 67, 70, 53, 56, 21, 10, 97, 75, 78, 105, 61, 64, 114, 83, 86, 98, 91, 94, 68,
    71, 37, 200, 26, 27, 38, 106, 192, 28, 39, 76, 79, 115, 84, 87, 201, 29, 40, 102, 99, 193, 69, 72, 92,
    95, 169, 110, 107, 77, 80, 137, 30, 31, 41, 42, 208, 117, 216, 88, 202, 145, 205, 122, 85, 224, 103, 100, 194,
    154, 93, 197, 96, 232, 111, 121, 108, 209, 172, 217, 225, 119, 140, 32, 240, 43, 203, 206, 233, 123, 248, 104, 101,
    195, 198, 148, 155, 124, 112, 109, 174, 210, 241, 213, 249, 142, 218, 204, 207, 221, 125, 226, 150, 130, 196, 199, 229,
    157, 113, 234, 126, 138, 176, 237, 211, 129, 242, 214, 146, 144, 245, 219, 127, 153, 250, 222, 162, 152, 253, 227, 159,
    161, 131, 230, 170, 128, 116, 235, 212, 312, 139, 238, 257, 215, 132, 243, 220, 280, 147, 246, 223, 156, 251, 228, 288,
    163, 254, 231, 164, 133, 265, 236, 264, 297, 171, 118, 239, 315, 141, 244, 272, 281, 258, 134, 247, 283, 149, 252, 256,
    289, 158, 255, 291, 165, 135, 266, 296, 273, 166, 120, 267, 173, 143, 298, 304, 305, 317, 136, 275, 260, 151, 282, 313,
    160, 167, 285, 290, 259, 168, 268, 299, 175, 177, 178, 269, 274, 293, 319, 262, 306, 300, 284, 307, 179, 185, 277, 314,
    186, 292, 180, 287, 261, 276, 187, 271, 301, 270, 302, 295, 308, 309, 286, 181, 279, 316, 294, 188, 263, 278, 303, 310,
    311, 318, 320, 321, 322, 328, 329, 182, 189, 335, 337, 323, 339, 330, 341, 324, 190, 331, 343, 183, 345, 336, 325, 191,
    332, 338, 184, 340, 326, 333, 342, 327, 334, 344, 346, 347, 348,
)


def kernel(
    tok, upw, dnw, cot, upp, dnp, own_out, far_out, ug_out, dg_out,
    T, G, U, D, DT, PS, XS, XR, RSS, RSR, AD, IG, RA, RB, CS, R1, R1B, RC, RD, CS2, R2, ZS, UG, DG,
    lsem, ags, agr, zxs, zxr, xss, xr, rss, rsr, ads, adr, acs, acr, igs, igr, zss, zsr,
):
    r = lax.axis_index("row")
    q = lax.axis_index("col")
    zl, c = r // 2, lax.rem(r, 2)
    zh = q // 16
    y = lax.rem(q // 4, 4)
    x = lax.rem(q, 4)
    oc = 1 - c

    def m4(v):
        return lax.rem(v, 4)

    xp = (r, zh * 16 + y * 4 + m4(x + 1))
    xm = (r, zh * 16 + y * 4 + m4(x + 3))
    yp = (r, zh * 16 + m4(y + 1) * 4 + x)
    ym = (r, zh * 16 + m4(y + 3) * 4 + x)
    zz = (r, (1 - zh) * 16 + y * 4 + x)
    co = (zl * 2 + oc, q)
    zp = (m4(zl + 1) * 2 + c, q)
    zm = (m4(zl + 3) * 2 + c, q)

    o0 = m4(x + y)
    locals_ = [
        pltpu.make_async_copy(tok, T.at[0, o0, :, y], lsem.at[0]),
        pltpu.make_async_copy(cot, G.at[0, o0, :, y], lsem.at[1]),
        pltpu.make_async_copy(upw, U, lsem.at[2]),
        pltpu.make_async_copy(dnw, D, lsem.at[3]),
    ]
    for d in locals_:
        d.start()

    barrier = pltpu.get_barrier_semaphore()
    for dev in (xp, xm, yp, ym, zz, co, zp, zm):
        pl.semaphore_signal(barrier, inc=1, device_id=dev, device_id_type=MESH)
    locals_[0].wait()
    locals_[1].wait()
    pl.semaphore_wait(barrier, 8)

    pending = []

    def rcopy(src, dst, ss, rs, dev):
        return pltpu.make_async_remote_copy(
            src_ref=src, dst_ref=dst, send_sem=ss, recv_sem=rs, device_id=dev, device_id_type=MESH
        )

    def send(make, cond=None):
        if cond is None:
            make().start()
        else:
            @pl.when(cond)
            def _():
                make().start()

    def arrive(ref, rs):
        rcopy(ref, ref, xss, rs, co).wait_recv()

    def sent(ref, ss, cond=None):
        pending.append((cond, lambda: rcopy(ref, ref, ss, zsr.at[0], co)))

    class Gather:
        def __init__(self, A, arr, rho):
            self.A, self.arr, self.rho = A, arr, rho
            self.fp, self.fm, self.sp, self.sm = (xp, xm, yp, ym) if arr == 0 else (yp, ym, xp, xm)
            sent(A.at[rho, 0, :, 0:3], ags.at[arr, rho, 0])
            sent(A.at[rho, 0:3], ags.at[arr, rho, 1])

        def ref(self, da, db, h=None):
            da, db = da % 4, db % 4
            xx, yy = (m4(x + da), m4(y + db)) if self.arr == 0 else (m4(x + db), m4(y + da))
            o = m4(xx + yy)
            if h is None:
                return self.A.at[self.rho, o, :, yy]
            return self.A.at[self.rho, o, h, yy]

        slots = {0: 0, 1: 1, 4: 2, 7: 2, 2: 3, 6: 4, 8: 5, 11: 6, 3: 7, 5: 7, 9: 7, 10: 7, 12: 8, 13: 8, 14: 8, 15: 8}

        def put(self, k, ref, dev):
            ss = ags.at[self.arr, self.rho, 0 if k in (0, 1, 4, 7) else 1]
            rs = agr.at[self.arr, self.rho, self.slots[k]]
            send(lambda: rcopy(ref, ref, ss, rs, dev))

        def get(self, k, ref):
            arrive(ref, agr.at[self.arr, self.rho, self.slots[k]])

        def start_a(self):
            own = self.ref(0, 0)
            self.put(0, own, self.fp)
            self.put(1, own, self.fm)

        def start_b(self):
            own = self.ref(0, 0)
            self.put(2, own, self.sp)
            self.put(3, own, self.sm)

        def step2a(self):
            self.get(0, self.ref(-1, 0))
            self.put(4, self.ref(-1, 0, 0), self.fp)
            self.get(1, self.ref(1, 0))
            self.put(7, self.ref(1, 0, 1), self.fm)

        def step2b(self):
            self.put(5, self.ref(-1, 0), self.sp)
            self.put(6, self.ref(-1, 0), self.sm)
            self.put(8, self.ref(1, 0), self.sp)
            self.put(9, self.ref(1, 0), self.sm)

        def step3(self):
            self.get(4, self.ref(2, 0))
            self.put(10, self.ref(2, 0), self.sp)
            self.put(11, self.ref(2, 0), self.sm)

        def step4a(self):
            self.get(2, self.ref(0, -1))
            self.put(12, self.ref(0, -1), self.sp)

        def step4b(self):
            self.get(6, self.ref(-1, 1))
            self.put(13, self.ref(-1, 1), self.sm)

        def step4c(self):
            self.get(8, self.ref(1, -1))
            self.put(14, self.ref(1, -1), self.sp)

        def step4d(self):
            self.get(11, self.ref(2, 1))
            self.put(15, self.ref(2, 1), self.sm)

        def near(self):
            self.get(3, self.A.at[self.rho, 0])

        def far(self):
            self.get(12, self.A.at[self.rho, 0])

    gt0, gg0 = Gather(T, 0, 0), Gather(G, 1, 0)
    gt1, gg1 = Gather(T, 0, 1), Gather(G, 1, 1)

    def across(A, k):
        src, dst = A.at[0, o0, :, y], A.at[1, o0, :, y]
        sent(src, zxs.at[k])
        send(lambda: rcopy(src, dst, zxs.at[k], zxr.at[k], zz))

    def across_wait(A, k):
        arrive(A.at[1, o0, :, y], zxr.at[k])

    shift = (0, 3, 1, 2)

    def slot(do):
        return m4(x + y + do)

    def shard_row(arr, g, do):
        if arr == 0:
            return m4(y + shift[g])
        return m4(slot(do) + 4 - m4(x + shift[g]))

    def row_a(rho, arr, g):
        A = G if arr else T
        t = jnp.concatenate([A[rho, slot(o), :, shard_row(arr, g, o)].reshape(32, 1536) for o in range(4)], axis=0)
        if arr == 0:
            p = jnp.dot(t, U[...], preferred_element_type=F32)
        else:
            p = jnp.dot(t, DT[...], preferred_element_type=F32)
        p = p.reshape(4, 2, 16, 768)
        for o in range(4):
            PS[rho, arr, slot(o), :, shard_row(arr, g, o)] = p[o]
        for o in range(4):
            XS[rho, arr, g, o] = PS[rho, arr, slot(o), oc, shard_row(arr, g, o)].astype(BF)
        send(lambda: rcopy(XS.at[rho, arr, g], XR.at[rho, arr, g], xss, xr.at[rho, arr, g], co))

    def block_of(way, j):
        return 2 + j if way == 0 else j

    def rs_pass(rho, arr, g, way):
        dev = zp if way == 0 else zm
        k = (rho, arr, g, way)
        return lambda: rcopy(RSS.at[k], RSR.at[k], rss.at[way], rsr.at[k], dev)

    def rs_arrive(rho, arr, g, way):
        k = (rho, arr, g, way)
        arrive(RSR.at[k], rsr.at[k])

    def row_b(rho, arr, g):
        arrive(XR.at[rho, arr, g], xr.at[rho, arr, g])
        for way, first in ((0, 0), (1, 3)):
            make = rs_pass(rho, arr, g, way)
            cond = zl == first
            for j in range(2):
                o = block_of(way, j)
                yy = shard_row(arr, g, o)
                s = PS[rho, arr, slot(o), c, yy] + XR[rho, arr, g, o].astype(F32)
                PS[rho, arr, slot(o), c, yy] = s

                @pl.when(cond)
                def _():
                    RSS[rho, arr, g, way, j] = s.astype(BF)

            send(make, cond)

    def row_c(rho, arr, g, hop, way):
        make = rs_pass(rho, arr, g, way)

        @pl.when(zl == (hop if way == 0 else 3 - hop))
        def _():
            rs_arrive(rho, arr, g, way)
            for j in range(2):
                o = block_of(way, j)
                s = PS[rho, arr, slot(o), c, shard_row(arr, g, o)] + RSR[rho, arr, g, way, j].astype(F32)
                RSS[rho, arr, g, way, j] = s.astype(BF)
            make().start()

    def row_sum(rho, arr, g, way):
        @pl.when(zl == (3 if way == 0 else 0))
        def _():
            rs_arrive(rho, arr, g, way)
            for j in range(2):
                o = block_of(way, j)
                yy = shard_row(arr, g, o)
                PS[rho, arr, slot(o), c, yy] = PS[rho, arr, slot(o), c, yy] + RSR[rho, arr, g, way, j].astype(F32)

    sent(XS, xss)
    sent(RSS.at[:, :, :, 0], rss.at[0], zl <= 2)
    sent(RSS.at[:, :, :, 1], rss.at[1], zl >= 1)
    sent(AD.at[:, 0:2, c], ads.at[0], zl <= 2)
    sent(AD.at[:, 2:4, c], ads.at[1], zl >= 1)
    sent(AD.at[:, :, c], acs)

    def ad_block(rho, o, yy, core):
        return AD.at[rho, o, core, yy]

    def ad_line(rho, way, k):
        dev = zp if way == 0 else zm
        ref = ad_block(rho, slot(block_of(1 - way, k // 4)), m4(y + k % 4), c)
        return lambda: rcopy(ref, ref, ads.at[way], adr.at[rho, way, k], dev)

    def ad_core(rho, o, yy):
        ref = ad_block(rho, o, yy, c)
        return lambda: rcopy(ref, ref, acs, acr.at[rho], co)

    def row_d(rho, k, way):
        o, yy = slot(block_of(way, k // 4)), m4(y + k % 4)
        line, core = ad_line(rho, 1 - way, k), ad_core(rho, o, yy)

        @pl.when(zl == (3 if way == 0 else 0))
        def _():
            pre = PS[rho, 0, o, c, yy]
            dact = PS[rho, 1, o, c, yy]
            cdf = 0.5 * (1.0 + lax.erf(pre * HALF_ROOT))
            dens = jnp.exp(-0.5 * pre * pre) * INV_ROOT_TAU
            AD[rho, o, c, yy, 0] = (pre * cdf).astype(BF)
            AD[rho, o, c, yy, 1] = (dact * (cdf + pre * dens)).astype(BF)
            line().start()
            core().start()

    def row_e(rho, k, hop, way):
        o, yy = slot(block_of(1 - way, k // 4)), m4(y + k % 4)
        line, core = ad_line(rho, way, k), ad_core(rho, o, yy)

        @pl.when(zl == (hop if way == 0 else 3 - hop))
        def _():
            arrive(ad_block(rho, o, yy, c), adr.at[rho, way, k])
            if hop < 3:
                line().start()
            core().start()

    def row_f(rho):
        arrive(AD.at[rho, :, oc], acr.at[rho])

    def ig_matmul(rho, h):
        @pl.loop(0, 3)
        def _(n):
            rows = pl.ds(pl.multiple_of(h * 768 + n * 256, 256), 256)
            cols = pl.ds(pl.multiple_of(n * 256, 256), 256)
            for o in range(0, 4, 2):
                dh = AD[rho, o:o + 2, :, :, 1].reshape(256, 768)
                acc = lax.dot_general(dh, U[rows, :], NT, preferred_element_type=F32)
                acc = acc.astype(BF).reshape(2, 2, 4, 16, 256)
                for oo in range(2):
                    for yy in range(4):
                        xx = (o + oo - yy) % 4
                        a, b = (yy, xx) if h == 0 else (xx, yy)
                        IG[rho, h, a, b, :, :, cols] = acc[oo, :, yy]

    class Scatter:
        def __init__(self, rho, h):
            self.rho, self.h = rho, h
            self.fp, self.fm, self.sp, self.sm = (yp, ym, xp, xm) if h == 0 else (xp, xm, yp, ym)
            self.a, self.b = (y, x) if h == 0 else (x, y)

            sent(IG.at[rho, h, 0:3], igs.at[rho, h, 0])
            sent(IG.at[rho, h, 0, 0:3], igs.at[rho, h, 1])

        slots = {0: 0, 1: 0, 2: 1, 3: 1, 4: 1, 5: 1, 6: 2, 7: 2, 8: 3, 9: 3, 10: 3, 11: 3}

        def put(self, k, src, dst, dev):
            ss, rs = igs.at[self.rho, self.h, 0 if k < 6 else 1], igr.at[self.rho, self.h, self.slots[k]]
            send(lambda: rcopy(src, dst, ss, rs, dev))

        def get(self, k, ref):
            arrive(ref, igr.at[self.rho, self.h, self.slots[k]])

        def start(self):
            i = (self.rho, self.h)
            a = self.a
            a2 = m4(a + 2)
            self.put(0, IG.at[i[0], i[1], a2, 0:2], RA.at[i[0], i[1], 0], self.fp)
            self.put(1, IG.at[i[0], i[1], a2, 2:4], RA.at[i[0], i[1], 1], self.fm)

        def start_b(self):
            i = (self.rho, self.h)
            a1, a3 = m4(self.a + 1), m4(self.a + 3)
            self.put(2, IG.at[i[0], i[1], a1, 2:4], RB.at[i[0], i[1], 0, 2:4], self.fp)
            self.put(3, IG.at[i[0], i[1], a3, 0:2], RB.at[i[0], i[1], 1, 0:2], self.fm)

        def step2(self):
            rho, h, a = self.rho, self.h, self.a
            a1, a3 = m4(a + 1), m4(a + 3)
            self.get(0, RA.at[rho, h])
            CS[rho, h, 0] = (IG[rho, h, a1, 0:2].astype(F32) + RA[rho, h, 0].astype(F32)).astype(BF)
            self.put(4, CS.at[rho, h, 0], RB.at[rho, h, 0, 0:2], self.fp)
            CS[rho, h, 1] = (IG[rho, h, a3, 2:4].astype(F32) + RA[rho, h, 1].astype(F32)).astype(BF)
            self.put(5, CS.at[rho, h, 1], RB.at[rho, h, 1, 2:4], self.fm)

        def step3(self):
            rho, h, a, b = self.rho, self.h, self.a, self.b
            self.get(2, RB.at[rho, h])
            for k in range(4):
                s = IG[rho, h, a, k].astype(F32) + RB[rho, h, 0, k].astype(F32) + RB[rho, h, 1, k].astype(F32)
                R1[rho, h, k] = s
                R1B[rho, h, k] = s.astype(BF)
            b1, b2, b3 = m4(b + 1), m4(b + 2), m4(b + 3)
            self.put(6, R1B.at[rho, h, b2, 0], RC.at[rho, h, 0], self.sp)
            self.put(7, R1B.at[rho, h, b2, 1], RC.at[rho, h, 1], self.sm)
            self.put(8, R1B.at[rho, h, b1, 1], RD.at[rho, h, 0, 1], self.sp)
            self.put(9, R1B.at[rho, h, b3, 0], RD.at[rho, h, 1, 0], self.sm)

        def step4(self):
            rho, h, b = self.rho, self.h, self.b
            b1, b3 = m4(b + 1), m4(b + 3)
            self.get(6, RC.at[rho, h])
            CS2[rho, h, 0] = (R1[rho, h, b1, 0] + RC[rho, h, 0].astype(F32)).astype(BF)
            self.put(10, CS2.at[rho, h, 0], RD.at[rho, h, 0, 0], self.sp)
            CS2[rho, h, 1] = (R1[rho, h, b3, 1] + RC[rho, h, 1].astype(F32)).astype(BF)
            self.put(11, CS2.at[rho, h, 1], RD.at[rho, h, 1, 1], self.sm)

        def step5(self):
            rho, h, b = self.rho, self.h, self.b
            self.get(8, RD.at[rho, h])
            s = R1[rho, h, b] + RD[rho, h, 0].astype(F32) + RD[rho, h, 1].astype(F32)
            cols = slice(h * 768, (h + 1) * 768)
            if rho == 0:
                R2[:, :, cols] = s
            else:
                ZS[h] = s.astype(BF)
                sent(ZS.at[h], zss.at[h])
                send(lambda: rcopy(ZS.at[h], far_out.at[:, :, cols], zss.at[h], zsr.at[h], zz))

        def out(self):
            h = self.h
            if h == 0:
                pltpu.make_async_copy(R2, own_out, lsem.at[0]).start()
            arrive(far_out.at[:, :, h * 768:(h + 1) * 768], zsr.at[h])

    sc = [[Scatter(rho, h) for h in range(2)] for rho in range(2)]

    def mask_weights():
        @pl.loop(0, 12)
        def _(i):
            rows = pl.ds(pl.multiple_of(i * 128, 128), 128)
            for j in range(6):
                cols = slice(j * 128, (j + 1) * 128)
                m = upp[j, i].astype(F32)
                U[rows, cols] = (U[rows, cols].astype(F32) * m).astype(BF)

        @pl.loop(0, 12)
        def _(i):
            cols = pl.ds(pl.multiple_of(i * 128, 128), 128)
            for j in range(6):
                rows = slice(j * 128, (j + 1) * 128)
                m = dnp[j, i].astype(F32)
                DT[cols, rows] = (D[rows, cols].astype(F32) * m).T.astype(BF)

    factor = 1.0 / 32.0

    def up_grads(lo, hi):
        @pl.loop(lo, hi)
        def _(n):
            cols = pl.ds(pl.multiple_of(n * 256, 256), 256)
            t = T[:, :, :, :, :, cols].reshape(1024, 256)
            for f in range(3):
                dh = AD[:, :, :, :, 1, :, f * 256:(f + 1) * 256].reshape(1024, 256)
                res = lax.dot_general(t, dh, TN, preferred_element_type=F32)
                for bi in range(2):
                    for bj in range(2):
                        m = upp[f * 2 + bj, n * 2 + bi].astype(F32) * factor
                        UG[
                            pl.ds(pl.multiple_of(n * 256 + bi * 128, 128), 128),
                            f * 256 + bj * 128:f * 256 + (bj + 1) * 128,
                        ] = (res[bi * 128:(bi + 1) * 128, bj * 128:(bj + 1) * 128] * m).astype(BF)

    def down_grads(lo, hi):
        @pl.loop(lo, hi)
        def _(n):
            cols = pl.ds(pl.multiple_of(n * 256, 256), 256)
            g = G[:, :, :, :, :, cols].reshape(1024, 256)
            for f in range(3):
                ac = AD[:, :, :, :, 0, :, f * 256:(f + 1) * 256].reshape(1024, 256)
                res = lax.dot_general(ac, g, TN, preferred_element_type=F32)
                for bi in range(2):
                    for bj in range(2):
                        m = dnp[f * 2 + bi, n * 2 + bj].astype(F32) * factor
                        DG[
                            f * 256 + bi * 128:f * 256 + (bi + 1) * 128,
                            pl.ds(pl.multiple_of(n * 256 + bj * 128, 128), 128),
                        ] = (res[bi * 128:(bi + 1) * 128, bj * 128:(bj + 1) * 128] * m).astype(BF)

    def put_up(lo, hi):
        up_grads(lo, hi)
        rows = slice(lo * 256, hi * 256)
        pltpu.make_async_copy(UG.at[rows], ug_out.at[rows], lsem.at[4]).start()

    def put_down(lo, hi):
        down_grads(lo, hi)
        cols = slice(lo * 256, hi * 256)
        pltpu.make_async_copy(DG.at[:, cols], dg_out.at[:, cols], lsem.at[5]).start()

    steps = {}

    def at(name, fn, *args):
        steps[name] = (fn, args)

    def weights():
        locals_[2].wait()
        locals_[3].wait()
        mask_weights()

    for name, gt in (("g0t", gt0), ("g0g", gg0), ("g1t", gt1), ("g1g", gg1)):
        for step in ("start_a", "start_b", "step2a", "step2b", "step3", "step4a", "step4b", "step4c", "step4d", "near", "far"):
            at(name + "_" + step, getattr(gt, step))
    at("acrossT", across, T, 0)
    at("acrossG", across, G, 1)
    at("weights", weights)
    at("awaitT", across_wait, T, 0)
    at("awaitG", across_wait, G, 1)
    for rho in range(2):
        for g in range(4):
            for arr in range(2):
                n = "%d%d%d" % (rho, arr, g)
                at("a" + n, row_a, rho, arr, g)
                at("b" + n, row_b, rho, arr, g)
                for way, w in enumerate("rl"):
                    at("c1" + w + n, row_c, rho, arr, g, 1, way)
                    at("c2" + w + n, row_c, rho, arr, g, 2, way)
                    at("s" + w + n, row_sum, rho, arr, g, way)
        for k in range(8):
            n = "%d%d" % (rho, k)
            at("dr" + n, row_d, rho, k, 0)
            at("dl" + n, row_d, rho, k, 1)
            for hop in (1, 2, 3):
                at("e%dl" % hop + n, row_e, rho, k, hop, 0)
                at("e%dr" % hop + n, row_e, rho, k, hop, 1)
        at("f%d" % rho, row_f, rho)
        for h in range(2):
            n = "%d%d" % (rho, h)
            at("ig" + n, ig_matmul, rho, h)
            at("st" + n, sc[rho][h].start)
            at("sb" + n, sc[rho][h].start_b)
            for k in (2, 3, 4, 5):
                at("s%d" % k + n, getattr(sc[rho][h], "step%d" % k))
    for k in range(6):
        at("up%d" % k, put_up, k, k + 1)
        at("dn%d" % k, put_down, k, k + 1)
    at("out0", sc[0][0].out)
    at("out1", sc[0][1].out)

    names = list(steps)
    assert sorted(ORDER) == list(range(len(names)))
    for name in (names[k] for k in ORDER):
        fn, args = steps[name]
        with jax.named_scope(name):
            fn(*args)

    with jax.named_scope("drain"):
        for cond, make in pending:
            if cond is None:
                make().wait_send()
            else:
                @pl.when(cond)
                def _():
                    make().wait_send()
    pltpu.make_async_copy(UG, ug_out, lsem.at[4]).wait()
    pltpu.make_async_copy(DG, dg_out, lsem.at[5]).wait()
    pltpu.make_async_copy(R2, own_out, lsem.at[0]).wait()


def on_device(tokens, up_weight, down_weight, cotangent, up_pattern, down_pattern):
    any_ = pl.BlockSpec(memory_space=pl.ANY)
    smem = pl.BlockSpec(memory_space=pltpu.SMEM)
    dma = pltpu.SemaphoreType.DMA
    V = pltpu.VMEM
    own, far, up_grad, down_grad = pl.pallas_call(
        kernel,
        out_shape=(
            jax.ShapeDtypeStruct((2, 16, 1536), F32),
            jax.ShapeDtypeStruct((2, 16, 1536), BF),
            jax.ShapeDtypeStruct((1536, 768), BF),
            jax.ShapeDtypeStruct((768, 1536), BF),
        ),
        in_specs=[any_, any_, any_, any_, smem, smem],
        out_specs=(any_, any_, any_, any_),
        scratch_shapes=[
            V((2, 4, 2, 4, 16, 1536), BF),
            V((2, 4, 2, 4, 16, 1536), BF),
            V((1536, 768), BF),
            V((768, 1536), BF),
            V((1536, 768), BF),
            V((2, 2, 4, 2, 4, 16, 768), F32),
            V((2, 2, 4, 4, 16, 768), BF),
            V((2, 2, 4, 4, 16, 768), BF),
            V((2, 2, 4, 2, 2, 16, 768), BF),
            V((2, 2, 4, 2, 2, 16, 768), BF),
            V((2, 4, 2, 4, 2, 16, 768), BF),
            V((2, 2, 4, 4, 2, 16, 768), BF),
            V((2, 2, 2, 2, 2, 16, 768), BF),
            V((2, 2, 2, 4, 2, 16, 768), BF),
            V((2, 2, 2, 2, 2, 16, 768), BF),
            V((2, 2, 4, 2, 16, 768), F32),
            V((2, 2, 4, 2, 16, 768), BF),
            V((2, 2, 2, 16, 768), BF),
            V((2, 2, 2, 2, 16, 768), BF),
            V((2, 2, 2, 16, 768), BF),
            V((2, 16, 1536), F32),
            V((2, 2, 16, 768), BF),
            V((1536, 768), BF),
            V((768, 1536), BF),
            dma((7,)),
            dma((2, 2, 2)), dma((2, 2, 9)),
            dma((2,)), dma((2,)),
            dma, dma((2, 2, 4)),
            dma((2,)), dma((2, 2, 4, 2)),
            dma((2,)), dma((2, 2, 8)),
            dma, dma((2,)),
            dma((2, 2, 2)), dma((2, 2, 4)),
            dma((2,)), dma((2,)),
        ],
        compiler_params=pltpu.CompilerParams(
            collective_id=0, has_side_effects=True, vmem_limit_bytes=62 * 1024 * 1024
        ),
    )(
        tokens.reshape(2, 16, 1536),
        up_weight,
        down_weight,
        cotangent.reshape(2, 16, 1536),
        up_pattern.T,
        down_pattern,
    )
    return ((own + far.astype(F32)).astype(BF).reshape(32, 1536), up_grad, down_grad)


def solution(mesh):
    return jax.shard_map(
        on_device,
        mesh=mesh,
        in_specs=(
            P("col", "row"),
            P("row", "col"),
            P("col", "row"),
            P("col", "row"),
            P("row", "col"),
            P("col", "row"),
        ),
        out_specs=(P("col", "row"), P("row", "col"), P("col", "row")),
        check_vma=False,
    )
```
